32 devices in a mesh: expert: 8 (over z, y), dp: 4 (over x, core).
Axes of the slice: x: 2, y: 2, z: 4, core: 2. Of those that a mesh axis runs over, the one named last changes fastest.
Arguments:
- tokens: bfloat16 [4096, 1664], P(('expert', 'dp')), may hold values from -6 to 6
- out_grad: bfloat16 [4096, 1664], P(('expert', 'dp')), may hold values from -6 to 6
- expert_index: int32 [4096, 2], P(('expert', 'dp')), may hold values from 0 to 7, as said below
- slots: int32 [4096, 2], P(('expert', 'dp')), may hold values from -1 to 23, as said below
- combine: bfloat16 [4096, 2], P(('expert', 'dp')), may hold values from 0.099609375 to 1
- w_in: bfloat16 [8, 1664, 4096], P('expert', None, 'dp'), may hold values from -0.15625 to 0.15625
- b_in: float32 [8, 4096], P('expert', 'dp'), may hold values from -3 to 3
- w_out: bfloat16 [8, 4096, 1664], P('expert', 'dp'), may hold values from -0.09375 to 0.09375
Outputs:
- d_tokens: bfloat16 [4096, 1664], P(('expert', 'dp'))
- grad_w_in: float32 [8, 1664, 4096], P('expert', None, 'dp')
- grad_w_out: float32 [8, 4096, 1664], P('expert', 'dp')
- grad_b_in: float32 [8, 4096], P('expert', 'dp')
The draws below stay inside these ranges and needn't reach their ends.
Inputs may be any that keep to these rules, and one draw needn't show every extreme that they name: `expert_index`: the two experts of a token differ. `slots`: a slot counts the earlier assignments to the same expert among the tokens of the same device, all first choices in token order before all second choices; it is -1 where that count reaches 24 (the assignment is dropped). So an expert takes at most 24 rows from one device, and in every draw some expert takes exactly 24 rows from every device.
All inputs are finite; a program needn't handle non-finite values.
Results may differ from the reference program's by a relative error of at most 0.01.
Values may be sent and summed in bfloat16 or wider, within the bound.
No kernel may reach another device: no remote copies, remote signals or barrier semaphores. Data moves between devices by JAX's collectives and lax.ppermute only.
A program may use at most 128 MiB of HBM per device.

```python
import jax
import jax.numpy as jnp
from jax import lax

D = 1664
FF = 4096
T_DEV = 128
EXPERTS = 8
CAP = 24
TOKENS = 4096
N_EXPERT = 8
N_DP = 4


def routing(key):
    blocks = TOKENS // T_DEV
    order = jax.random.permutation(jax.random.fold_in(key, 101), EXPERTS)
    draw_one = jax.random.randint(jax.random.fold_in(key, 102), (blocks, T_DEV), 0, EXPERTS)
    draw_two = jax.random.randint(jax.random.fold_in(key, 103), (blocks, T_DEV), 0, EXPERTS)
    rank_first = jnp.minimum(draw_one, draw_two)
    scores = jax.random.randint(jax.random.fold_in(key, 104), (blocks, T_DEV), 0, 1048576)
    scores = scores * T_DEV + jnp.arange(T_DEV, dtype=jnp.int32)[None, :]
    position = jnp.argsort(jnp.argsort(scores, axis=1, stable=True), axis=1, stable=True)
    rank_first = jnp.where(position < CAP, 0, rank_first)
    offset = jax.random.randint(jax.random.fold_in(key, 105), (blocks, T_DEV), 1, EXPERTS)
    rank_second = (rank_first + offset) % EXPERTS
    first = order[rank_first]
    second = order[rank_second]
    chosen = jnp.stack([first, second], axis=-1)
    flat = jnp.concatenate([first, second], axis=1)
    onehot = (flat[..., None] == jnp.arange(EXPERTS, dtype=jnp.int32)[None, None, :]).astype(jnp.int32)
    before = jnp.cumsum(onehot, axis=1) - onehot
    rank = jnp.sum(before * onehot, axis=-1)
    place = jnp.where(rank < CAP, rank, -1)
    places = jnp.stack([place[:, :T_DEV], place[:, T_DEV:]], axis=-1)
    return (chosen.reshape(TOKENS, 2).astype(jnp.int32), places.reshape(TOKENS, 2).astype(jnp.int32))


def draw_expert_index(key, part):
    return routing(key)[0]


def draw_slots(key, part):
    return routing(key)[1]


def levels(own_key, extent, shards, least, top_value):
    factor_of, own = 1.0, jax.random.fold_in(own_key, 6)
    for dim, parts in shards:
        draws = jnp.exp(jax.random.uniform(jax.random.fold_in(own, dim), (parts,), jnp.float32, least / len(shards), top_value / len(shards)))
        factor_of = factor_of * jnp.repeat(draws, extent[dim] // parts).reshape([-1 if axis == dim else 1 for axis in range(len(extent))])
    return factor_of


def gaussian(key, shape, spread, limit, split=(), kind=jnp.bfloat16):
    values = spread * jax.random.normal(key, shape, jnp.float32)
    if split:
        values = values * levels(key, shape, split, -0.22, 0.18)
    return jnp.clip(values, -limit, limit).astype(kind)


def setup_inputs(seed: int = 0) -> dict:
    streams_of = jax.random.split(jax.random.key(seed), 9)
    return {
        "tokens": gaussian(streams_of[0], (TOKENS, D), 1.0, 6.0, ((0, 32),)),
        "out_grad": gaussian(streams_of[1], (TOKENS, D), 1.0, 6.0, ((0, 32),)),
        "expert_index": draw_expert_index(jax.random.fold_in(streams_of[8], 71), 0),
        "slots": draw_slots(jax.random.fold_in(streams_of[8], 71), 0),
        "combine": jnp.clip(0.099609375 + 0.9003906 * jax.random.uniform(streams_of[4], (TOKENS, 2), jnp.float32) ** levels(streams_of[4], (TOKENS, 2), ((0, 32),), -0.2, 0.2), 0.099609375, 1.0).astype(jnp.bfloat16),
        "w_in": gaussian(streams_of[5], (EXPERTS, D, FF), D ** -0.5, 0.15625, ((0, 8), (2, 4))),
        "b_in": gaussian(streams_of[6], (EXPERTS, FF), 0.5, 3.0, ((0, 8), (1, 4)), jnp.float32),
        "w_out": gaussian(streams_of[7], (EXPERTS, FF, D), FF ** -0.5, 0.09375, ((0, 8), (1, 4))),
    }


inv_root_two = 0.7071067811865476
inv_root_two_pi = 0.3989422804014327


def gelu_value(values):
    return 0.5 * values * (1.0 + lax.erf(values * inv_root_two))


def gelu_slope(values):
    normal_cdf = 0.5 * (1.0 + lax.erf(values * inv_root_two))
    density = jnp.exp(-0.5 * values * values) * inv_root_two_pi
    return normal_cdf + values * density


def reference(tokens, out_grad, expert_index, slots, combine, w_in, b_in, w_out):
    shape_four = (N_EXPERT, N_DP, T_DEV)
    inputs = tokens.reshape(shape_four + (D,))
    grads = out_grad.astype(jnp.float32).reshape(shape_four + (D,))
    weights = combine.astype(jnp.float32).reshape(shape_four + (2,))
    chosen = expert_index.reshape(shape_four + (2,))
    places = slots.reshape(shape_four + (2,))
    scaled_first = (weights[..., 0:1] * grads).astype(jnp.bfloat16).astype(jnp.float32)
    scaled_second = (weights[..., 1:2] * grads).astype(jnp.bfloat16).astype(jnp.float32)
    slot_ids = jnp.arange(CAP, dtype=jnp.int32)
    shard_width = FF // N_DP

    def one_expert(expert):
        def picks(member):
            same_expert = (chosen[..., member] == expert)[:, :, None, :]
            same_slot = places[..., member][:, :, None, :] == slot_ids[None, None, :, None]
            return (same_expert & same_slot).astype(jnp.float32)

        pick_first = picks(0)
        pick_second = picks(1)
        rows_x = jnp.einsum("srct,srtd->rscd", pick_first + pick_second, inputs.astype(jnp.float32))
        rows_x = rows_x.astype(jnp.bfloat16).reshape(-1, D)
        rows_g = jnp.einsum("srct,srtd->rscd", pick_first, scaled_first)
        rows_g = rows_g + jnp.einsum("srct,srtd->rscd", pick_second, scaled_second)
        rows_g = rows_g.astype(jnp.bfloat16).reshape(-1, D)
        first_w = w_in[expert]
        second_w = w_out[expert]
        pre_act = jnp.dot(rows_x, first_w, preferred_element_type=jnp.float32) + b_in[expert]
        hidden = gelu_value(pre_act).astype(jnp.bfloat16)
        grad_second = jnp.dot(hidden.T, rows_g, preferred_element_type=jnp.float32)
        d_hidden = jnp.dot(rows_g, second_w.T, preferred_element_type=jnp.float32)
        d_pre = (d_hidden * gelu_slope(pre_act)).astype(jnp.bfloat16)
        grad_bias = jnp.sum(d_pre.astype(jnp.float32), axis=0)
        grad_first = jnp.dot(rows_x.T, d_pre, preferred_element_type=jnp.float32)
        summed = jnp.zeros((rows_x.shape[0], D), jnp.float32)
        for shard in range(N_DP):
            lower = shard * shard_width
            upper = lower + shard_width
            partial_rows = jnp.dot(d_pre[:, lower:upper], first_w[:, lower:upper].T, preferred_element_type=jnp.float32)
            summed = summed + lax.optimization_barrier(partial_rows.astype(jnp.bfloat16)).astype(jnp.float32)
        d_rows = summed.astype(jnp.bfloat16).reshape(N_DP, N_EXPERT, CAP, D)
        return grad_first, grad_second, grad_bias, d_rows

    grad_w_in, grad_w_out, grad_b_in, d_rows = lax.map(one_expert, jnp.arange(EXPERTS, dtype=jnp.int32))
    source_ids = jnp.arange(N_EXPERT, dtype=jnp.int32)[:, None, None]
    replica_ids = jnp.arange(N_DP, dtype=jnp.int32)[None, :, None]
    result = jnp.zeros(shape_four + (D,), jnp.float32)
    for member in range(2):
        place = places[..., member]
        safe_place = jnp.maximum(place, 0).astype(jnp.int32)
        picked = d_rows[chosen[..., member], replica_ids, source_ids, safe_place].astype(jnp.float32)
        result = result + picked * (place >= 0).astype(jnp.float32)[..., None]
    d_tokens = result.astype(jnp.bfloat16).reshape(TOKENS, D)
    return d_tokens, grad_w_in, grad_w_out, grad_b_in
```

```python
import jax
import jax.numpy as jnp
from jax import lax
from jax.sharding import PartitionSpec as P

inv_root_two = 0.7071067811865476
inv_root_two_pi = 0.3989422804014327


def swap(value, axis, mask):
    size = lax.axis_size(axis)
    return lax.ppermute(value, axis, [(i, i ^ mask) for i in range(size)])


def joined(pieces):
    return pieces[0] if len(pieces) == 1 else jnp.concatenate(pieces, axis=0)


def picks(expert_index, slots, expert_ids, capacity):
    expert_ids = expert_ids[:, None, None]
    slot_ids = jnp.arange(capacity, dtype=jnp.int32)[None, :, None]
    return [
        (expert_index[None, None, :, k] == expert_ids) & (slots[None, None, :, k] == slot_ids)
        for k in range(2)
    ]


def on_device(tokens, out_grad, expert_index, slots, combine, w_in, b_in, w_out):
    experts = lax.axis_size("expert")
    tok_count, width = tokens.shape
    capacity = max(2, (3 * tok_count + 2 * experts - 1) // (2 * experts))
    me = lax.axis_index("expert")
    first_w, second_w, bias = w_in[0], w_out[0], b_in[0]

    order = jnp.bitwise_xor(me, jnp.arange(experts, dtype=jnp.int32))
    pick = picks(expert_index, slots, order, capacity)
    chosen = (pick[0] | pick[1]).astype(jnp.bfloat16).reshape(experts * capacity, tok_count)
    scale = sum(
        jnp.sum(jnp.where(pick[k], combine[None, None, :, k].astype(jnp.float32), 0.0), axis=-1)
        for k in range(2)
    ).reshape(experts * capacity, 1)
    rows_x = jnp.dot(chosen, tokens, preferred_element_type=jnp.float32).astype(jnp.bfloat16)
    rows_g = jnp.dot(chosen, out_grad, preferred_element_type=jnp.float32)
    rows_g = (rows_g * scale).astype(jnp.bfloat16)
    rows = jnp.concatenate([rows_x, rows_g], axis=1)

    def block(k):
        return rows[k * capacity : (k + 1) * capacity]

    across_masks = [2 << i for i in range(lax.axis_size("dp").bit_length() - 2)]
    half, quarter = experts // 2, experts // 4
    near = list(range(half))
    far_one = list(range(half, half + quarter))
    far_two = list(range(half + quarter, experts))
    got = {0: block(0)}
    for k in far_one + near[1:]:
        got[k] = swap(block(k), "expert", k)
    late = rows[(half + quarter) * capacity :]
    late, got[half - 1] = lax.optimization_barrier((late, got[half - 1]))
    for i, k in enumerate(far_two):
        got[k] = swap(late[i * capacity : (i + 1) * capacity], "expert", k)

    groups = [[0], near[1:], far_one, far_two]
    sets = []
    for group in groups:
        pieces = [joined([got[k] for k in group])]
        for mask in across_masks:
            pieces = pieces + [swap(piece, "dp", mask) for piece in pieces]
        sets.append(pieces + [swap(piece, "dp", 1) for piece in pieces])
    sets = [[jnp.concatenate([a, b]) for a, b in zip(sets[0], sets[1])]] + sets[2:]

    hidden_parts, slope_parts, row_parts, back = [], [], [], []
    for pieces in sets:
        chunk = jnp.concatenate(pieces)
        x, g = chunk[:, :width], chunk[:, width:]
        pre_act = jnp.dot(x, first_w, preferred_element_type=jnp.float32) + bias
        cdf = 0.5 * (1.0 + lax.erf(pre_act * inv_root_two))
        hidden = (pre_act * cdf).astype(jnp.bfloat16)
        density = jnp.exp(-0.5 * pre_act * pre_act) * inv_root_two_pi
        d_hidden = lax.dot_general(
            g, second_w, (((1,), (1,)), ((), ())), preferred_element_type=jnp.float32
        )
        d_pre = (d_hidden * (cdf + pre_act * density)).astype(jnp.bfloat16)
        term = lax.dot_general(
            d_pre, first_w, (((1,), (1,)), ((), ())), preferred_element_type=jnp.float32
        ).astype(jnp.bfloat16)
        hidden_parts.append(hidden)
        slope_parts.append(d_pre)
        row_parts.append(chunk)
        for mask in [1] + across_masks[::-1]:
            kept = term.shape[0] // 2
            arrived = swap(term[kept:], "dp", mask)
            term = (term[:kept].astype(jnp.float32) + arrived.astype(jnp.float32)).astype(jnp.bfloat16)
        back.append(term)

    returned = []
    for group, rows_back in zip([near, far_one, far_two], back):
        for i, k in enumerate(group):
            part = rows_back[i * capacity : (i + 1) * capacity]
            returned.append(part if k == 0 else swap(part, "expert", k))
    returned = jnp.concatenate(returned)
    d_tokens = lax.dot_general(
        chosen, returned, (((0,), (0,)), ((), ())), preferred_element_type=jnp.float32
    )

    hidden = jnp.concatenate(hidden_parts)
    d_pre = jnp.concatenate(slope_parts)
    rows_all = jnp.concatenate(row_parts)
    grad_second = lax.dot_general(
        hidden, rows_all[:, width:], (((0,), (0,)), ((), ())), preferred_element_type=jnp.float32
    )
    grad_first = lax.dot_general(
        rows_all[:, :width], d_pre, (((0,), (0,)), ((), ())), preferred_element_type=jnp.float32
    )
    grad_bias = jnp.sum(d_pre.astype(jnp.float32), axis=0)
    return (d_tokens.astype(jnp.bfloat16), grad_first[None], grad_second[None], grad_bias[None])


def solution(mesh):
    in_specs = (
        P(("expert", "dp"), None),
        P(("expert", "dp"), None),
        P(("expert", "dp"), None),
        P(("expert", "dp"), None),
        P(("expert", "dp"), None),
        P("expert", None, "dp"),
        P("expert", "dp"),
        P("expert", "dp", None),
    )
    out_specs = (
        P(("expert", "dp"), None),
        P("expert", None, "dp"),
        P("expert", "dp", None),
        P("expert", "dp"),
    )
    return jax.shard_map(
        on_device, mesh=mesh, in_specs=in_specs, out_specs=out_specs, check_vma=False
    )
```

```python
import functools

import jax
import jax.numpy as jnp
from jax import lax
from jax.experimental import pallas as pl
from jax.experimental.pallas import tpu as pltpu
from jax.sharding import PartitionSpec as P

inv_root_two = 0.7071067811865476
inv_root_two_pi = 0.3989422804014327


def swap(value, axis, mask):
    size = lax.axis_size(axis)
    return lax.ppermute(value, axis, [(i, i ^ mask) for i in range(size)])


def joined(pieces):
    return pieces[0] if len(pieces) == 1 else jnp.concatenate(pieces, axis=0)


def after(value, *needed):
    return lax.optimization_barrier((value,) + needed)[0]


def dispatch_kernel(capacity, me, tokens, out_grad, index, slots, weights, rows, chosen, *scratch):
    held, sems = scratch[:-1], scratch[-1]
    copies = [
        pltpu.make_async_copy(source, target, sems.at[i])
        for i, (source, target) in enumerate(zip((index, slots, weights, tokens, out_grad), held))
    ]
    for copy in copies:
        copy.start()
    index_held, slots_held, weights_held, tokens_held, grad_held = held
    count, tok_count = chosen.shape
    width = tokens.shape[1]
    row = lax.broadcasted_iota(jnp.int32, (count, tok_count), 0)
    step = ((row.astype(jnp.float32) + 0.5) * (1.0 / capacity)).astype(jnp.int32)
    slot = row - step * capacity
    expert = step ^ me[0]
    for copy in copies[:3]:
        copy.wait()
    taken = [
        (index_held[k : k + 1, :] == expert) & (slots_held[k : k + 1, :] == slot) for k in range(2)
    ]
    weight = weights_held[...].astype(jnp.float32)
    scale = sum(jnp.where(taken[k], weight[k : k + 1, :], 0.0) for k in range(2))
    scale = jnp.sum(scale, axis=1, keepdims=True)
    one_hot = jnp.where(taken[0] | taken[1], 1.0, 0.0).astype(jnp.bfloat16)
    chosen[...] = one_hot
    copies[3].wait()
    picked = jnp.dot(one_hot, tokens_held[...], preferred_element_type=jnp.float32)
    rows[:, :width] = picked.astype(jnp.bfloat16)
    copies[4].wait()
    picked = jnp.dot(one_hot, grad_held[...], preferred_element_type=jnp.float32)
    rows[:, width:] = (picked * scale).astype(jnp.bfloat16)


def dispatch_call(capacity, me, tokens, out_grad, index, slots, weights):
    tok_count, width = tokens.shape
    count = lax.axis_size("expert") * capacity
    arrays = (index, slots, weights, tokens, out_grad)
    in_vmem = pl.BlockSpec(memory_space=pltpu.VMEM)
    return pl.pallas_call(
        functools.partial(dispatch_kernel, capacity),
        out_shape=[
            jax.ShapeDtypeStruct((count, 2 * width), jnp.bfloat16),
            jax.ShapeDtypeStruct((count, tok_count), jnp.bfloat16),
        ],
        in_specs=[pl.BlockSpec(memory_space=pltpu.SMEM)] + [pl.BlockSpec(memory_space=pltpu.HBM)] * 5,
        out_specs=[in_vmem] * 2,
        scratch_shapes=[pltpu.VMEM(x.shape, x.dtype) for x in arrays]
        + [pltpu.SemaphoreType.DMA((5,))],
        compiler_params=pltpu.CompilerParams(vmem_limit_bytes=16 << 20),
        cost_estimate=pl.CostEstimate(flops=0, bytes_accessed=0, transcendentals=0),
    )(me, tokens, out_grad, index, slots, weights)


contract_last = (((1,), (1,)), ((), ()))


def chunk_kernel(step, rows, w_in, bias, w_out, hidden, d_pre, kept, leaving, total):
    width, units = w_in.shape
    half = kept.shape[0]
    ones = jnp.ones((8, rows.shape[0]), jnp.bfloat16)
    for j in range(0, units, step):
        part = slice(j, j + step)
        pre_act = jnp.dot(rows[:, :width], w_in[:, part], preferred_element_type=jnp.float32)
        pre_act = pre_act + bias[:, part]
        d_hidden = lax.dot_general(
            rows[:, width:], w_out[part, :], contract_last, preferred_element_type=jnp.float32
        )
        cdf = 0.5 * (1.0 + lax.erf(pre_act * inv_root_two))
        hidden[:, part] = (pre_act * cdf).astype(jnp.bfloat16)
        density = jnp.exp(-0.5 * pre_act * pre_act) * inv_root_two_pi
        d_pre[:, part] = (d_hidden * (cdf + pre_act * density)).astype(jnp.bfloat16)
        total[:, part] = jnp.dot(ones, d_pre[:, part], preferred_element_type=jnp.float32)
    term = lax.dot_general(
        d_pre[...], w_in[...], contract_last, preferred_element_type=jnp.float32
    ).astype(jnp.bfloat16)
    kept[...] = term[:half]
    leaving[...] = term[half:]


def chunk_call(rows, w_in, bias, w_out):
    count = rows.shape[0]
    width, units = w_in.shape
    in_vmem = pl.BlockSpec(memory_space=pltpu.VMEM)
    shapes = [(count, units), (count, units), (count // 2, width), (count // 2, width)]
    return pl.pallas_call(
        functools.partial(chunk_kernel, min(512, units)),
        out_shape=[jax.ShapeDtypeStruct(shape, jnp.bfloat16) for shape in shapes]
        + [jax.ShapeDtypeStruct((8, units), jnp.float32)],
        in_specs=[in_vmem] * 4,
        out_specs=[in_vmem] * 5,
        compiler_params=pltpu.CompilerParams(vmem_limit_bytes=24 << 20),
        cost_estimate=pl.CostEstimate(flops=0, bytes_accessed=0, transcendentals=0),
    )(rows, w_in, bias, w_out)


def on_device(tokens, out_grad, expert_index, slots, combine, w_in, b_in, w_out):
    experts = lax.axis_size("expert")
    tok_count, width = tokens.shape
    capacity = max(2, (3 * tok_count + 2 * experts - 1) // (2 * experts))
    me = lax.axis_index("expert")
    first_w, second_w = w_in[0], w_out[0]

    rows, chosen = dispatch_call(
        capacity, me.reshape(1), tokens, out_grad, expert_index.T, slots.T, combine.T
    )

    def block(k):
        return rows[k * capacity : (k + 1) * capacity]

    across_masks = [2 << i for i in range(lax.axis_size("dp").bit_length() - 2)]
    half, quarter = experts // 2, experts // 4
    def spread(value):
        pieces = [value]
        for mask in across_masks:
            pieces = pieces + [swap(piece, "dp", mask) for piece in pieces]
        return pieces

    near, far_one, far_two = range(half), range(half, half + quarter), range(half + quarter, experts)
    got = {0: block(0)}
    for k in range(1, experts):
        got[k] = swap(block(k), "expert", k)
    groups = [near, far_one, far_two]
    runs = [[near], [far_one], [far_two]]
    sets = [[spread(joined([got[k] for k in run])) for run in part] for part in runs]
    columns = []
    for part in sets:
        columns.append(joined([run[i] for i in range(len(part[0])) for run in part]))

    made = []
    for column in columns:
        rows_all = jnp.concatenate([column, swap(column, "dp", 1)])
        made.append((rows_all,) + tuple(chunk_call(rows_all, first_w, b_in, second_w)))
    row_parts, hidden_parts, slope_parts = [[m[i] for m in made] for i in range(3)]

    def first_sum(kept, leaving):
        return (kept.astype(jnp.float32) + swap(leaving, "dp", 1).astype(jnp.float32)).astype(jnp.bfloat16)

    def rest_sum(term, *needed):
        for mask in across_masks[::-1]:
            middle = term.shape[0] // 2
            arrived = swap(term[middle:], "dp", mask)
            if needed:
                arrived = after(arrived, *needed)
            term = (term[:middle].astype(jnp.float32) + arrived.astype(jnp.float32)).astype(jnp.bfloat16)
        return term

    sums = [first_sum(m[3], m[4]) for m in made]
    far_back = [rest_sum(sums[i], made[0][3]) for i in (1, 2)]
    hidden_parts[0] = after(hidden_parts[0], sums[0], far_back[0])
    hidden = jnp.concatenate(hidden_parts)
    rows_all = jnp.concatenate(row_parts)
    grad_second = lax.dot_general(
        hidden, rows_all[:, width:], (((0,), (0,)), ((), ())), preferred_element_type=jnp.float32
    )
    near_back = rest_sum(sums[0], grad_second)
    def part(value, i):
        return value[i * capacity : (i + 1) * capacity]

    returned = {}
    for group, value in zip((far_one, far_two), far_back):
        for i, k in enumerate(group):
            leaving = part(value, i)
            if k in far_one or k in far_two:
                leaving = after(leaving, sums[0])
            returned[k] = swap(leaving, "expert", k)
    slope_parts[0] = after(slope_parts[0], near_back, *[returned[k] for k in far_one])
    d_pre = jnp.concatenate(slope_parts)
    grad_first = lax.dot_general(
        rows_all[:, :width], d_pre, (((0,), (0,)), ((), ())), preferred_element_type=jnp.float32
    )

    returned[0] = part(near_back, 0)
    for k in range(1, half):
        leaving = part(near_back, k)
        if k > 1:
            leaving = after(leaving, returned[half + (k - 2) % quarter])
        returned[k] = swap(leaving, "expert", k)
    returned = jnp.concatenate([returned[k] for k in range(experts)])
    d_tokens = lax.dot_general(
        chosen, returned, (((0,), (0,)), ((), ())), preferred_element_type=jnp.float32
    )
    grad_bias = sum(m[5][:1] for m in made)
    return (d_tokens.astype(jnp.bfloat16), grad_first[None], grad_second[None], grad_bias)


def solution(mesh):
    in_specs = (
        P(("expert", "dp"), None),
        P(("expert", "dp"), None),
        P(("expert", "dp"), None),
        P(("expert", "dp"), None),
        P(("expert", "dp"), None),
        P("expert", None, "dp"),
        P("expert", "dp"),
        P("expert", "dp", None),
    )
    out_specs = (
        P(("expert", "dp"), None),
        P("expert", None, "dp"),
        P("expert", "dp", None),
        P("expert", "dp"),
    )
    return jax.shard_map(
        on_device, mesh=mesh, in_specs=in_specs, out_specs=out_specs, check_vma=False
    )
```

```python
import functools

import jax
import jax.numpy as jnp
from jax import lax
from jax.experimental import pallas as pl
from jax.experimental.pallas import tpu as pltpu
from jax.sharding import PartitionSpec as P

inv_root_two = 0.7071067811865476
inv_root_two_pi = 0.3989422804014327


def swap(value, axis, mask):
    size = lax.axis_size(axis)
    return lax.ppermute(value, axis, [(i, i ^ mask) for i in range(size)])


def joined(pieces):
    return pieces[0] if len(pieces) == 1 else jnp.concatenate(pieces, axis=0)


def after(value, *needed):
    return lax.optimization_barrier((value,) + needed)[0]


def dispatch_kernel(capacity, me, tokens, out_grad, index, slots, weights, chosen, *refs):
    blocks, held, sems = refs[:-6], refs[-6:-1], refs[-1]
    copies = [
        pltpu.make_async_copy(source, target, sems.at[i])
        for i, (source, target) in enumerate(zip((index, slots, weights, tokens, out_grad), held))
    ]
    for copy in copies:
        copy.start()
    index_held, slots_held, weights_held, tokens_held, grad_held = held
    count, tok_count = chosen.shape
    width = tokens.shape[1]
    row = lax.broadcasted_iota(jnp.int32, (count, tok_count), 0)
    step = ((row.astype(jnp.float32) + 0.5) * (1.0 / capacity)).astype(jnp.int32)
    slot = row - step * capacity
    expert = step ^ me[0]
    for copy in copies[:3]:
        copy.wait()
    taken = [
        (index_held[k : k + 1, :] == expert) & (slots_held[k : k + 1, :] == slot) for k in range(2)
    ]
    weight = weights_held[...].astype(jnp.float32)
    scale = sum(jnp.where(taken[k], weight[k : k + 1, :], 0.0) for k in range(2))
    scale = jnp.sum(scale, axis=1, keepdims=True)
    one_hot = jnp.where(taken[0] | taken[1], 1.0, 0.0).astype(jnp.bfloat16)
    chosen[...] = one_hot
    copies[3].wait()
    picked = jnp.dot(one_hot, tokens_held[...], preferred_element_type=jnp.float32)
    for k, block in enumerate(blocks):
        block[:, :width] = picked[k * capacity : (k + 1) * capacity].astype(jnp.bfloat16)
    copies[4].wait()
    picked = jnp.dot(one_hot, grad_held[...], preferred_element_type=jnp.float32)
    picked = (picked * scale).astype(jnp.bfloat16)
    for k, block in enumerate(blocks):
        block[:, width:] = picked[k * capacity : (k + 1) * capacity]


def dispatch_call(capacity, me, tokens, out_grad, index, slots, weights):
    tok_count, width = tokens.shape
    count = lax.axis_size("expert") * capacity
    arrays = (index, slots, weights, tokens, out_grad)
    in_vmem = pl.BlockSpec(memory_space=pltpu.VMEM)
    return pl.pallas_call(
        functools.partial(dispatch_kernel, capacity),
        out_shape=[
            jax.ShapeDtypeStruct((count, tok_count), jnp.bfloat16),
        ]
        + [jax.ShapeDtypeStruct((capacity, 2 * width), jnp.bfloat16)] * lax.axis_size("expert"),
        in_specs=[pl.BlockSpec(memory_space=pltpu.SMEM)] + [pl.BlockSpec(memory_space=pl.ANY)] * 5,
        out_specs=[in_vmem] * (1 + lax.axis_size("expert")),
        scratch_shapes=[pltpu.VMEM(x.shape, x.dtype) for x in arrays]
        + [pltpu.SemaphoreType.DMA((5,))],
        compiler_params=pltpu.CompilerParams(vmem_limit_bytes=58 << 20),
        cost_estimate=pl.CostEstimate(flops=0, bytes_accessed=0, transcendentals=0),
    )(me, tokens, out_grad, index, slots, weights)


contract_last = (((1,), (1,)), ((), ()))


def chunk_kernel(step, rows, w_in, bias, w_out, hidden, d_pre, kept, leaving, total):
    width, units = w_in.shape
    half = kept.shape[0]
    ones = jnp.ones((8, rows.shape[0]), jnp.bfloat16)
    for j in range(0, units, step):
        part = slice(j, j + step)
        pre_act = jnp.dot(rows[:, :width], w_in[:, part], preferred_element_type=jnp.float32)
        pre_act = pre_act + bias[:, part]
        d_hidden = lax.dot_general(
            rows[:, width:], w_out[part, :], contract_last, preferred_element_type=jnp.float32
        )
        cdf = 0.5 * (1.0 + lax.erf(pre_act * inv_root_two))
        hidden[:, part] = (pre_act * cdf).astype(jnp.bfloat16)
        density = jnp.exp(-0.5 * pre_act * pre_act) * inv_root_two_pi
        d_pre[:, part] = (d_hidden * (cdf + pre_act * density)).astype(jnp.bfloat16)
        total[:, part] = jnp.dot(ones, d_pre[:, part], preferred_element_type=jnp.float32)
    term = lax.dot_general(
        d_pre[...], w_in[...], contract_last, preferred_element_type=jnp.float32
    ).astype(jnp.bfloat16)
    kept[...] = term[:half]
    leaving[...] = term[half:]


def chunk_call(rows, w_in, bias, w_out):
    count = rows.shape[0]
    width, units = w_in.shape
    in_vmem = pl.BlockSpec(memory_space=pltpu.VMEM)
    shapes = [(count, units), (count, units), (count // 2, width), (count // 2, width)]
    return pl.pallas_call(
        functools.partial(chunk_kernel, min(512, units)),
        out_shape=[jax.ShapeDtypeStruct(shape, jnp.bfloat16) for shape in shapes]
        + [jax.ShapeDtypeStruct((8, units), jnp.float32)],
        in_specs=[in_vmem] * 4,
        out_specs=[in_vmem] * 5,
        compiler_params=pltpu.CompilerParams(vmem_limit_bytes=24 << 20),
        cost_estimate=pl.CostEstimate(flops=0, bytes_accessed=0, transcendentals=0),
    )(rows, w_in, bias, w_out)


def on_device(tokens, out_grad, expert_index, slots, combine, w_in, b_in, w_out):
    experts = lax.axis_size("expert")
    tok_count, width = tokens.shape
    capacity = max(2, (3 * tok_count + 2 * experts - 1) // (2 * experts))
    me = lax.axis_index("expert")
    first_w, second_w = w_in[0], w_out[0]

    chosen, *sent = dispatch_call(
        capacity, me.reshape(1), tokens, out_grad, expert_index.T, slots.T, combine.T
    )

    across_masks = [2 << i for i in range(lax.axis_size("dp").bit_length() - 2)]
    half, quarter = experts // 2, experts // 4
    def spread(value):
        pieces = [value]
        for mask in across_masks:
            pieces = pieces + [swap(piece, "dp", mask) for piece in pieces]
        return pieces

    near, far_one, far_two = range(half), range(half, half + quarter), range(half + quarter, experts)
    got = {0: sent[0]}
    for k in range(1, experts):
        got[k] = swap(sent[k], "expert", k)
    groups = [near, far_one, far_two]
    runs = [[near], [far_one], [far_two]]
    sets = [[spread(joined([got[k] for k in run])) for run in part] for part in runs]
    columns = []
    for part in sets:
        columns.append(joined([run[i] for i in range(len(part[0])) for run in part]))

    made = []
    for column in columns:
        rows_all = jnp.concatenate([column, swap(column, "dp", 1)])
        made.append((rows_all,) + tuple(chunk_call(rows_all, first_w, b_in, second_w)))
    row_parts, hidden_parts, slope_parts = [[m[i] for m in made] for i in range(3)]

    def first_sum(kept, leaving):
        return (kept.astype(jnp.float32) + swap(leaving, "dp", 1).astype(jnp.float32)).astype(jnp.bfloat16)

    def rest_sum(term, *needed):
        for mask in across_masks[::-1]:
            middle = term.shape[0] // 2
            arrived = swap(term[middle:], "dp", mask)
            if needed:
                arrived = after(arrived, *needed)
            term = (term[:middle].astype(jnp.float32) + arrived.astype(jnp.float32)).astype(jnp.bfloat16)
        return term

    sums = [first_sum(m[3], m[4]) for m in made]
    far_back = [rest_sum(sums[i], made[0][3]) for i in (1, 2)]
    hidden_parts[0] = after(hidden_parts[0], sums[0], far_back[0])
    hidden = jnp.concatenate(hidden_parts)
    rows_all = jnp.concatenate(row_parts)
    grad_second = lax.dot_general(
        hidden, rows_all[:, width:], (((0,), (0,)), ((), ())), preferred_element_type=jnp.float32
    )
    near_back = rest_sum(sums[0], grad_second)
    def part(value, i):
        return value[i * capacity : (i + 1) * capacity]

    returned = {}
    for group, value in zip((far_one, far_two), far_back):
        for i, k in enumerate(group):
            leaving = part(value, i)
            if k in far_one or k in far_two:
                leaving = after(leaving, sums[0])
            returned[k] = swap(leaving, "expert", k)
    slope_parts[0] = after(slope_parts[0], near_back, *[returned[k] for k in far_one])
    d_pre = jnp.concatenate(slope_parts)
    grad_first = lax.dot_general(
        rows_all[:, :width], d_pre, (((0,), (0,)), ((), ())), preferred_element_type=jnp.float32
    )

    returned[0] = part(near_back, 0)
    for k in range(1, half):
        leaving = part(near_back, k)
        if k > 1:
            leaving = after(leaving, returned[half + (k - 2) % quarter])
        returned[k] = swap(leaving, "expert", k)
    returned = jnp.concatenate([returned[k] for k in range(experts)])
    d_tokens = lax.dot_general(
        chosen, returned, (((0,), (0,)), ((), ())), preferred_element_type=jnp.float32
    )
    grad_bias = sum(m[5][:1] for m in made)
    return (d_tokens.astype(jnp.bfloat16), grad_first[None], grad_second[None], grad_bias)


def solution(mesh):
    in_specs = (
        P(("expert", "dp"), None),
        P(("expert", "dp"), None),
        P(("expert", "dp"), None),
        P(("expert", "dp"), None),
        P(("expert", "dp"), None),
        P("expert", None, "dp"),
        P("expert", "dp"),
        P("expert", "dp", None),
    )
    out_specs = (
        P(("expert", "dp"), None),
        P("expert", None, "dp"),
        P("expert", "dp", None),
        P("expert", "dp"),
    )
    return jax.shard_map(
        on_device, mesh=mesh, in_specs=in_specs, out_specs=out_specs, check_vma=False
    )
```

```python
import functools

import jax
import jax.numpy as jnp
from jax import lax
from jax.experimental import pallas as pl
from jax.experimental.pallas import tpu as pltpu
from jax.sharding import PartitionSpec as P

inv_root_two = 0.7071067811865476
inv_root_two_pi = 0.3989422804014327


def swap(value, axis, mask):
    size = lax.axis_size(axis)
    return lax.ppermute(value, axis, [(i, i ^ mask) for i in range(size)])


def joined(pieces):
    return pieces[0] if len(pieces) == 1 else jnp.concatenate(pieces, axis=0)


def after(value, *needed):
    return lax.optimization_barrier((value,) + needed)[0]


def dispatch_kernel(capacity, me, tokens, out_grad, index, slots, weights, chosen, *refs):
    blocks, held, sems = refs[:-6], refs[-6:-1], refs[-1]
    copies = [
        pltpu.make_async_copy(source, target, sems.at[i])
        for i, (source, target) in enumerate(zip((index, slots, weights, tokens, out_grad), held))
    ]
    for copy in copies:
        copy.start()
    index_held, slots_held, weights_held, tokens_held, grad_held = held
    count, tok_count = chosen.shape
    width = tokens.shape[1]
    row = lax.broadcasted_iota(jnp.int32, (count, tok_count), 0)
    step = ((row.astype(jnp.float32) + 0.5) * (1.0 / capacity)).astype(jnp.int32)
    slot = row - step * capacity
    expert = step ^ me[0]
    for copy in copies[:3]:
        copy.wait()
    taken = [
        (index_held[k : k + 1, :] == expert) & (slots_held[k : k + 1, :] == slot) for k in range(2)
    ]
    weight = weights_held[...].astype(jnp.float32)
    scale = sum(jnp.where(taken[k], weight[k : k + 1, :], 0.0) for k in range(2))
    scale = jnp.sum(scale, axis=1, keepdims=True)
    one_hot = jnp.where(taken[0] | taken[1], 1.0, 0.0).astype(jnp.bfloat16)
    chosen[...] = one_hot
    copies[3].wait()
    picked = jnp.dot(one_hot, tokens_held[...], preferred_element_type=jnp.float32)
    for k, block in enumerate(blocks):
        block[:, :width] = picked[k * capacity : (k + 1) * capacity].astype(jnp.bfloat16)
    copies[4].wait()
    picked = jnp.dot(one_hot, grad_held[...], preferred_element_type=jnp.float32)
    picked = (picked * scale).astype(jnp.bfloat16)
    for k, block in enumerate(blocks):
        block[:, width:] = picked[k * capacity : (k + 1) * capacity]


def dispatch_call(capacity, me, tokens, out_grad, index, slots, weights):
    tok_count, width = tokens.shape
    count = lax.axis_size("expert") * capacity
    arrays = [
        pltpu.with_memory_space_constraint(x, pltpu.HBM)
        for x in (index, slots, weights, tokens, out_grad)
    ]
    in_vmem = pl.BlockSpec(memory_space=pltpu.VMEM)
    return pl.pallas_call(
        functools.partial(dispatch_kernel, capacity),
        out_shape=[
            jax.ShapeDtypeStruct((count, tok_count), jnp.bfloat16),
        ]
        + [jax.ShapeDtypeStruct((capacity, 2 * width), jnp.bfloat16)] * lax.axis_size("expert"),
        in_specs=[pl.BlockSpec(memory_space=pltpu.SMEM)] + [pl.BlockSpec(memory_space=pltpu.HBM)] * 5,
        out_specs=[in_vmem] * (1 + lax.axis_size("expert")),
        scratch_shapes=[pltpu.VMEM(x.shape, x.dtype) for x in arrays]
        + [pltpu.SemaphoreType.DMA((5,))],
        compiler_params=pltpu.CompilerParams(vmem_limit_bytes=16 << 20),
        cost_estimate=pl.CostEstimate(flops=0, bytes_accessed=0, transcendentals=0),
    )(me, arrays[3], arrays[4], *arrays[:3])


contract_last = (((1,), (1,)), ((), ()))


def chunk_kernel(step, rows, w_in, bias, w_out, before, hidden, d_pre, kept, leaving, total):
    width, units = w_in.shape
    half = kept.shape[0]
    ones = jnp.ones((8, rows.shape[0]), jnp.bfloat16)
    for j in range(0, units, step):
        part = slice(j, j + step)
        pre_act = jnp.dot(rows[:, :width], w_in[:, part], preferred_element_type=jnp.float32)
        pre_act = pre_act + bias[:, part]
        d_hidden = lax.dot_general(
            rows[:, width:], w_out[part, :], contract_last, preferred_element_type=jnp.float32
        )
        cdf = 0.5 * (1.0 + lax.erf(pre_act * inv_root_two))
        hidden[:, part] = (pre_act * cdf).astype(jnp.bfloat16)
        density = jnp.exp(-0.5 * pre_act * pre_act) * inv_root_two_pi
        d_pre[:, part] = (d_hidden * (cdf + pre_act * density)).astype(jnp.bfloat16)
        added = jnp.dot(ones, d_pre[:, part], preferred_element_type=jnp.float32)
        total[:, part] = before[:, part] + added[:1]
    term = lax.dot_general(
        d_pre[...], w_in[...], contract_last, preferred_element_type=jnp.float32
    ).astype(jnp.bfloat16)
    kept[...] = term[:half]
    leaving[...] = term[half:]


def chunk_call(rows, w_in, bias, w_out, before):
    count = rows.shape[0]
    width, units = w_in.shape
    in_vmem = pl.BlockSpec(memory_space=pltpu.VMEM)
    shapes = [(count, units), (count, units), (count // 2, width), (count // 2, width)]
    return pl.pallas_call(
        functools.partial(chunk_kernel, min(512, units)),
        out_shape=[jax.ShapeDtypeStruct(shape, jnp.bfloat16) for shape in shapes]
        + [jax.ShapeDtypeStruct((1, units), jnp.float32)],
        in_specs=[in_vmem] * 5,
        out_specs=[in_vmem] * 5,
        compiler_params=pltpu.CompilerParams(vmem_limit_bytes=24 << 20),
        cost_estimate=pl.CostEstimate(flops=0, bytes_accessed=0, transcendentals=0),
    )(rows, w_in, bias, w_out, before)


def on_device(tokens, out_grad, expert_index, slots, combine, w_in, b_in, w_out):
    experts = lax.axis_size("expert")
    tok_count, width = tokens.shape
    capacity = max(2, (3 * tok_count + 2 * experts - 1) // (2 * experts))
    me = lax.axis_index("expert")
    first_w, second_w = w_in[0], w_out[0]

    chosen, *sent = dispatch_call(
        capacity, me.reshape(1), tokens, out_grad, expert_index.T, slots.T, combine.T
    )

    across_masks = [2 << i for i in range(lax.axis_size("dp").bit_length() - 2)]
    half, quarter = experts // 2, experts // 4
    def spread(value):
        pieces = [value]
        for mask in across_masks:
            pieces = pieces + [swap(piece, "dp", mask) for piece in pieces]
        return pieces

    near, far_one, far_two = range(half), range(half, half + quarter), range(half + quarter, experts)
    got = {0: sent[0]}
    for k in range(1, experts):
        got[k] = swap(sent[k], "expert", k)
    groups = [near, far_one, far_two]
    runs = [[near], [far_one], [far_two]]
    sets = [[spread(joined([got[k] for k in run])) for run in part] for part in runs]
    columns = []
    for part in sets:
        columns.append(joined([run[i] for i in range(len(part[0])) for run in part]))

    made = [None] * len(columns)
    total = jnp.zeros((1, second_w.shape[0]), jnp.float32)
    for index in (1, 2, 0):
        column = columns[index]
        rows_all = jnp.concatenate([column, swap(column, "dp", 1)])
        made[index] = (rows_all,) + tuple(chunk_call(rows_all, first_w, b_in, second_w, total))
        total = made[index][5]

    row_parts, hidden_parts, slope_parts = [[m[i] for m in made] for i in range(3)]

    def first_sum(kept, leaving):
        return (kept.astype(jnp.float32) + swap(leaving, "dp", 1).astype(jnp.float32)).astype(jnp.bfloat16)

    def rest_sum(term, *needed):
        for mask in across_masks[::-1]:
            middle = term.shape[0] // 2
            arrived = swap(term[middle:], "dp", mask)
            if needed:
                arrived = after(arrived, *needed)
            term = (term[:middle].astype(jnp.float32) + arrived.astype(jnp.float32)).astype(jnp.bfloat16)
        return term

    sums = [first_sum(m[3], m[4]) for m in made]
    far_back = [rest_sum(sums[i], made[0][3]) for i in (1, 2)]
    hidden_parts[0] = after(hidden_parts[0], sums[0], far_back[0])
    hidden = jnp.concatenate(hidden_parts)
    rows_all = jnp.concatenate(row_parts)
    grad_second = lax.dot_general(
        hidden, rows_all[:, width:], (((0,), (0,)), ((), ())), preferred_element_type=jnp.float32
    )
    near_back = rest_sum(sums[0], grad_second)
    def part(value, i):
        return value[i * capacity : (i + 1) * capacity]

    returned = {}
    for group, value in zip((far_one, far_two), far_back):
        for i, k in enumerate(group):
            leaving = part(value, i)
            if k in far_one or k in far_two:
                leaving = after(leaving, sums[0])
            returned[k] = swap(leaving, "expert", k)
    slope_parts[0] = after(slope_parts[0], near_back, *[returned[k] for k in far_one])
    d_pre = jnp.concatenate(slope_parts)
    grad_first = lax.dot_general(
        rows_all[:, :width], d_pre, (((0,), (0,)), ((), ())), preferred_element_type=jnp.float32
    )

    returned[0] = part(near_back, 0)
    for k in range(1, half):
        leaving = part(near_back, k)
        if k > 1:
            leaving = after(leaving, returned[half + (k - 2) % quarter])
        returned[k] = swap(leaving, "expert", k)
    returned = jnp.concatenate([returned[k] for k in range(experts)])
    d_tokens = lax.dot_general(
        chosen, returned, (((0,), (0,)), ((), ())), preferred_element_type=jnp.float32
    )
    grad_bias = total
    return (d_tokens.astype(jnp.bfloat16), grad_first[None], grad_second[None], grad_bias)


def solution(mesh):
    in_specs = (
        P(("expert", "dp"), None),
        P(("expert", "dp"), None),
        P(("expert", "dp"), None),
        P(("expert", "dp"), None),
        P(("expert", "dp"), None),
        P("expert", None, "dp"),
        P("expert", "dp"),
        P("expert", "dp", None),
    )
    out_specs = (
        P(("expert", "dp"), None),
        P("expert", None, "dp"),
        P("expert", "dp", None),
        P("expert", "dp"),
    )
    return jax.shard_map(
        on_device, mesh=mesh, in_specs=in_specs, out_specs=out_specs, check_vma=False
    )
```
